256 devices in a mesh: grp: 8 (over x, y_hi), row: 32 (over y_lo, z, core).
Axes of the slice: x: 4, y: 4 (y_hi: 2, y_lo: 2; y = y_hi * 2 + y_lo), z: 8, core: 2. Of those that a mesh axis runs over, the one named last changes fastest.
Arguments:
- blocks: bfloat16 [256, 8, 10, 256, 256], P(('grp', 'row')), may hold values from 0 to 1
- columns: int32 [256, 8, 10], P(('grp', 'row')), may hold values from -1 to 255, as said below
- factor: bfloat16 [64, 65536], P(None, ('grp', 'row')), may hold values from 0 to 0.3, as said below
Outputs:
- updated: float32 [64, 65536], P(None, ('grp', 'row'))
The draws below stay inside these ranges and needn't reach their ends.
Inputs may be any that keep to these rules, and one draw needn't show every extreme that they name: Tile row i lies in group g = i // 32. In block h of tile row i the live slots come first and name distinct tile columns of group h (h * 32 to h * 32 + 31), none above i; block g always names i itself; blocks h > g are empty; a block holds at most 10 live slots, and -1 marks an empty slot. `factor`: entries are nonnegative.
All inputs are finite; a program needn't handle non-finite values.
Results may differ from the reference program's by a relative error of at most 0.0003.
Values may be sent and summed in bfloat16 or wider, within the bound.
A program may use at most 128 MiB of HBM per device.

```python
import jax
import jax.numpy as jnp
from jax import lax

TILE = 256
RANK = 64
SG = 10
GROUPS = 8
ROWS_GRP = 32
NT = 256
NODES = 65536


def draw_columns(key, part):
    row_ids = jnp.arange(NT).astype(jnp.int32)
    group_of = (row_ids // ROWS_GRP)[:, None, None]
    place_of = (row_ids % ROWS_GRP)[:, None, None]
    group_ids = jnp.arange(GROUPS).astype(jnp.int32)[None, :, None]
    offsets = jnp.arange(ROWS_GRP).astype(jnp.int32)[None, None, :]
    allowed = jnp.where(group_ids < group_of, ROWS_GRP, jnp.where(group_ids == group_of, place_of + 1, 0))
    scores = jax.random.randint(jax.random.fold_in(key, 7), (NT, GROUPS, ROWS_GRP), 0, 1 << 20) * ROWS_GRP + offsets
    invalid = (group_ids == group_of) & (offsets > place_of)
    scores = jnp.where(invalid, 1 << 30, scores)
    scores = jnp.where((group_ids == group_of) & (offsets == place_of), -1, scores)
    ordered = jnp.argsort(scores, axis=-1, stable=True).astype(jnp.int32)
    slot_ids = jnp.arange(SG).astype(jnp.int32)
    picked = jnp.take(ordered, jnp.minimum(slot_ids, ROWS_GRP - 1), axis=2)
    live_count = jnp.minimum(allowed[:, :, 0], SG)
    is_live = slot_ids[None, None, :] < live_count[:, :, None]
    group_start = (jnp.arange(GROUPS).astype(jnp.int32) * ROWS_GRP)[None, :, None]
    return jnp.where(is_live, group_start + picked, -1).astype(jnp.int32)


def draw_factor(key, part):
    base = jax.random.uniform(jax.random.fold_in(key, 11), (RANK, NODES), jnp.float32)
    tile_pos = (jnp.arange(NODES) // TILE).astype(jnp.float32) / (NT - 1)
    rising = 1.0 + 0.8 * tile_pos
    values = 0.08 * base * rising[None, :]
    return values.astype(jnp.bfloat16)


def block_levels(rng, dims, cuts, low, largest):
    loudness, own = 1.0, jax.random.fold_in(rng, 6)
    for position, shards_of in cuts:
        steps = jnp.exp(jax.random.uniform(jax.random.fold_in(own, position), (shards_of,), jnp.float32, low / len(cuts), largest / len(cuts)))
        loudness = loudness * jnp.repeat(steps, dims[position] // shards_of).reshape([-1 if axis == position else 1 for axis in range(len(dims))])
    return loudness


def setup_inputs(seed: int = 0) -> dict:
    arg_keys = jax.random.split(jax.random.key(seed), 4)
    blocks = jnp.clip(1.0 * jax.random.uniform(arg_keys[0], (NT, GROUPS, SG, TILE, TILE), jnp.float32) ** block_levels(arg_keys[0], (NT, GROUPS, SG, TILE, TILE), ((0, 256),), -0.2, 0.2), 0.0, 1.0).astype(jnp.bfloat16)
    columns = draw_columns(jax.random.fold_in(arg_keys[3], 71), 0)
    factor = draw_factor(jax.random.fold_in(arg_keys[3], 71), 0)
    return dict(blocks=blocks, columns=columns, factor=factor)


floor_value = 1e-6


def sweep(current, products, gram):
    def update(column, current):
        weights = lax.dynamic_index_in_dim(gram, column, 1, keepdims=False)
        fitted = jnp.dot(weights, current, precision=lax.Precision.HIGHEST)
        target = lax.dynamic_index_in_dim(products, column, 0, keepdims=False)
        present = lax.dynamic_index_in_dim(current, column, 0, keepdims=False)
        diagonal = gram[column, column]
        fresh = jnp.maximum(present + (target - fitted) / diagonal, floor_value)
        return lax.dynamic_update_index_in_dim(current, fresh, column, 0)

    return lax.fori_loop(0, current.shape[0], update, current)


def reference(blocks, columns, factor):
    rank_count, node_count = factor.shape
    tile_size = blocks.shape[-1]
    tile_rows = node_count // tile_size
    slabs = factor.astype(jnp.float32).reshape(rank_count, tile_rows, tile_size).transpose(1, 0, 2)
    row_blocks_all = blocks.reshape(tile_rows, -1, tile_size, tile_size)
    row_cols_all = columns.reshape(tile_rows, -1)

    def one_row(products, inputs):
        row_blocks, row_cols, row_index = inputs
        is_live = (row_cols >= 0).astype(jnp.float32)
        clipped = jnp.where(row_cols >= 0, row_cols, 0).astype(jnp.int32)
        values = row_blocks.astype(jnp.float32)
        fetched = slabs[clipped] * is_live[:, None, None]
        lower_part = jnp.einsum('srv,suv->ru', fetched, values, precision=lax.Precision.HIGHEST)
        own_slab = slabs[row_index]
        mirror = jnp.einsum('ru,suv->srv', own_slab, values, precision=lax.Precision.HIGHEST)
        mirror = mirror * is_live[:, None, None]
        products = products.at[clipped].add(mirror)
        products = products.at[row_index].add(lower_part)
        return products, None

    start_products = jnp.zeros((tile_rows, rank_count, tile_size), jnp.float32)
    indices = jnp.arange(tile_rows).astype(jnp.int32)
    products, _ = lax.scan(one_row, start_products, (row_blocks_all, row_cols_all, indices))
    products = products.transpose(1, 0, 2).reshape(rank_count, node_count)
    gram = jnp.dot(factor, factor.T, preferred_element_type=jnp.float32)
    return sweep(factor.astype(jnp.float32), products, gram)
```

```python
import functools

import jax
import jax.numpy as jnp
from jax import lax
from jax.experimental import pallas as pl
from jax.experimental.pallas import tpu as pltpu
from jax.sharding import Mesh
from jax.sharding import PartitionSpec as P

AXES = ("grp_0", "grp_1", "row_0", "row_1", "row_2")
BY_MESH = pl.DeviceIdType.MESH
LANES = 128
INV_LANE = 32
LEVELS = 65534.0
OFFSET = 32768.0
floor_value = 1e-6


def nt_dot(a, b):
    return lax.dot_general(a, b, (((1,), (1,)), ((), ())), preferred_element_type=jnp.float32)


def to_column(row, rank):
    spread = jnp.broadcast_to(row, (rank, LANES))
    lane = lax.broadcasted_iota(jnp.int32, (rank, LANES), 1)
    place = lax.broadcasted_iota(jnp.int32, (rank, LANES), 0)
    return jnp.sum(jnp.where(lane == place, spread, 0.0), axis=1, keepdims=True)


def exchange_kernel(
    sizes,
    blocks,
    cols,
    factor,
    prod_out,
    gram_out,
    tiles,
    hall,
    tab,
    tabin,
    tabs,
    sums,
    sumsin,
    scale,
    base,
    sendm,
    recvm,
    ownm,
    sendl,
    recvl,
    lower,
    gsend,
    grecv,
    part,
    cbuf,
    crecv,
    yrecv,
    zrecv,
    blk_sem,
    tab_sem,
    ag_s,
    ag_r,
    tab_s,
    tab_r,
    sum_s,
    sum_r,
    m_s,
    m_r,
    l_s,
    l_r,
    g_s,
    g_r,
    c_s,
    c_r,
    y_s,
    y_r,
    z_s,
    z_r,
):
    _, ngy, nry, nrz, nrc = sizes
    gx, gy, ry, rz, rc = [lax.axis_index(axis) for axis in AXES]
    groups, slots = tiles.shape[0], tiles.shape[1]
    rank, tile = factor.shape
    rows_grp = nry * nrz * nrc
    me = gx * ngy + gy

    def place(y, z, c):
        return (y * nrz + z) * nrc + c

    mine = place(ry, rz, rc)

    def group_peer(h):
        hx, hy = h // ngy, h % ngy
        flip = (hy - gy) * (hy - gy)
        return (hx, hy, ry + flip - 2 * ry * flip, rz, rc)

    def z_peer(z):
        return (gx, gy, ry, z, rc)

    y_peer = (gx, gy, 1 - ry, rz, rc)
    c_peer = (gx, gy, ry, rz, 1 - rc)

    def z_other(i):
        step = (i // 2 + 1) * (1 - 2 * (i % 2))
        return (rz + step + nrz) % nrz

    def remote(src, dst, send, recv, peer):
        return pltpu.make_async_remote_copy(
            src_ref=src, dst_ref=dst, send_sem=send, recv_sem=recv, device_id=peer, device_id_type=BY_MESH
        )

    def block_copy(h):
        return pltpu.make_async_copy(blocks.at[0, h], tiles.at[h], blk_sem.at[h])

    def loop(start, stop, body):
        def step(i, carry):
            body(i)
            return carry

        lax.fori_loop(start, stop, step, 0)

    loop(0, me + 1, lambda h: block_copy(h).start())

    hall[mine] = factor[...]
    hall[rows_grp] = jnp.zeros((rank, tile), hall.dtype)
    ownm[slots] = jnp.zeros((rank, tile), jnp.float32)
    for g in range(groups):
        recvm[g, slots] = jnp.full((rank, tile), -OFFSET, jnp.float32).astype(jnp.int32).astype(recvm.dtype)
    all_cols = cols[0]
    lane = lax.broadcasted_iota(jnp.int32, (groups, LANES), 1)
    row = lax.broadcasted_iota(jnp.int32, (groups, LANES), 0)
    table = jnp.where(lane >= INV_LANE, slots, rows_grp)
    for s in range(slots):
        column = jnp.broadcast_to(all_cols[:, s : s + 1], (groups, LANES))
        offset = column - row * rows_grp
        live = (offset >= 0) & (offset < rows_grp)
        table = jnp.where(live & (lane == s), offset, table)
        table = jnp.where(live & (lane - INV_LANE == offset), s, table)
    for h in range(groups):
        tab[h] = jnp.broadcast_to(table[h : h + 1], (8, LANES))
        tabin[h] = jnp.zeros((8, LANES), jnp.int32)
    tabin[me] = tab[me]
    row_sums = nt_dot(jnp.ones((8, tile), jnp.bfloat16), factor[...])
    sums[...] = jnp.zeros((8, LANES), jnp.float32)
    sums[:, 0:rank] = jnp.maximum(row_sums, 1e-30)
    to_levels = LEVELS / to_column(sums[0:1, :], rank)

    barrier = pltpu.get_barrier_semaphore()

    def greet(peer):
        pl.semaphore_signal(barrier, inc=1, device_id=peer, device_id_type=BY_MESH)

    loop(0, me, lambda h: greet(group_peer(h)))
    loop(me + 1, groups, lambda h: greet(group_peer(h)))
    loop(0, nrz - 1, lambda i: greet(z_peer(z_other(i))))
    greet(y_peer)
    greet(c_peer)
    pl.semaphore_wait(barrier, groups - 1 + nrz - 1 + 2)

    def z_send(z):
        return remote(factor, hall.at[mine], ag_s.at[z], ag_r.at[mine], z_peer(z))

    def y_send(z, src):
        p = place(ry, z, rc)
        return remote(src, hall.at[p], ag_s.at[nrz + z], ag_r.at[p], y_peer)

    def c_send(y, z, src):
        p = place(y, z, rc)
        return remote(src, hall.at[p], ag_s.at[2 * nrz + y * nrz + z], ag_r.at[p], c_peer)

    def arrived(p):
        remote(factor, hall.at[p], ag_s.at[0], ag_r.at[p], c_peer).wait_recv()

    loop(0, nrz - 1, lambda i: z_send(z_other(i)).start())
    y_send(rz, factor).start()
    c_send(ry, rz, factor).start()

    def table_send(h):
        return remote(tab.at[h], tabin.at[me], tab_s.at[h], tab_r.at[me], group_peer(h))

    def sums_send(h):
        return remote(sums, sumsin.at[me], sum_s.at[h], sum_r.at[me], group_peer(h))

    def small_sends(h):
        table_send(h).start()
        sums_send(h).start()

    loop(0, me, small_sends)

    def mirror_send(h):
        return remote(
            sendm.at[h], recvm.at[me, pl.ds(0, slots)], m_s.at[h], m_r.at[me], group_peer(h)
        )

    def mirror(h):
        block_copy(h).wait()
        for s in range(slots):
            product = jnp.dot(factor[...], tiles[h, s], preferred_element_type=jnp.float32)
            coded = jnp.round(product * to_levels - OFFSET)
            sendm[h, s] = coded.astype(jnp.int32).astype(sendm.dtype)
        mirror_send(h).start()

    def forward(i):
        z = z_other(i)
        p = place(ry, z, rc)
        arrived(p)
        y_send(z, hall.at[p]).start()
        c_send(ry, z, hall.at[p]).start()

    def first_step(i):
        @pl.when(i < me)
        def _():
            mirror(i)

        @pl.when(i < nrz - 1)
        def _():
            forward(i)

    loop(0, max(groups - 1, nrz - 1), first_step)

    def second_step(i):
        z = (rz + i) % nrz
        p = place(1 - ry, z, rc)
        arrived(p)
        c_send(1 - ry, z, hall.at[p]).start()

    loop(0, nrz, second_step)

    def tables_in(g):
        remote(tab.at[0], tabin.at[g], tab_s.at[0], tab_r.at[g], c_peer).wait_recv()
        remote(sums, sumsin.at[g], sum_s.at[0], sum_r.at[g], c_peer).wait_recv()
        column = to_column(sumsin[g][0:1, :], rank) * (1.0 / LEVELS)
        scale[g] = jnp.broadcast_to(column, (rank, tile))

    loop(me + 1, groups, tables_in)
    to_scalars = pltpu.make_async_copy(tabin, tabs, tab_sem)
    to_scalars.start()
    to_scalars.wait()
    loop(0, nry * nrz, lambda j: arrived(j * nrc + 1 - rc))

    def lower_send(g):
        return remote(sendl.at[g], recvl.at[me], l_s.at[g], l_r.at[me], group_peer(g))

    def serve(g):
        for s in range(slots):
            sendl[g, s] = hall[tabs[g, 0, s]]
        lower_send(g).start()

    loop(me + 1, groups, serve)

    def gram_step(p, total):
        return total + nt_dot(hall[p], hall[p])

    group_gram = lax.fori_loop(0, rows_grp, gram_step, jnp.zeros((rank, rank), jnp.float32))
    gsend[...] = jnp.zeros((rank, LANES), jnp.float32)
    gsend[:, 0:rank] = group_gram
    grecv[me] = gsend[...]

    block_copy(me).wait()
    lower[...] = jnp.zeros((rank, tile), jnp.float32)
    for s in range(slots):
        ownm[s] = jnp.dot(factor[...], tiles[me, s], preferred_element_type=jnp.float32)
        lower[...] += nt_dot(hall[tabs[me, 0, s]], tiles[me, s])

    def gram_send(h):
        return remote(gsend, grecv.at[me], g_s.at[h], g_r.at[me], group_peer(h))

    loop(0, me, lambda h: gram_send(h).start())
    loop(me + 1, groups, lambda h: gram_send(h).start())

    base[...] = jnp.zeros((rank, tile), jnp.float32)

    def mirror_in(g):
        remote(sendm.at[0], recvm.at[g, pl.ds(0, slots)], m_s.at[0], m_r.at[g], c_peer).wait_recv()
        base[...] += OFFSET * scale[g]

    loop(me + 1, groups, mirror_in)

    def summed(p):
        def add(g, total):
            coded = recvm[g, tabs[g, 0, INV_LANE + p]].astype(jnp.int32).astype(jnp.float32)
            return total + coded * scale[g]

        return lax.fori_loop(me + 1, groups, add, base[...] + ownm[tabs[me, 0, INV_LANE + p]])

    def core_send(j):
        return remote(cbuf.at[j], crecv.at[j], c_s.at[j], c_r.at[j], c_peer)

    def for_other(j):
        cbuf[j] = summed(j * nrc + 1 - rc)
        core_send(j).start()

    def for_this(j):
        part[j] = summed(j * nrc + rc)

    loop(0, nry * nrz, for_other)
    loop(0, nry * nrz, for_this)

    def row_y_send(z):
        return remote(part.at[(1 - ry) * nrz + z], yrecv.at[z], y_s.at[z], y_r.at[z], y_peer)

    def to_y(i):
        z = (rz + i) % nrz
        j = (1 - ry) * nrz + z
        core_send(j).wait_recv()
        part[j] += crecv[j]
        row_y_send(z).start()

    loop(0, nrz, to_y)

    def row_z_send(z):
        return remote(part.at[ry * nrz + z], zrecv.at[rz], z_s.at[z], z_r.at[rz], z_peer(z))

    def to_z(z):
        j = ry * nrz + z
        core_send(j).wait_recv()
        row_y_send(z).wait_recv()
        part[j] += crecv[j] + yrecv[z]

    def to_z_sent(i):
        z = z_other(i)
        to_z(z)
        row_z_send(z).start()

    loop(0, nrz - 1, to_z_sent)
    to_z(rz)

    def lower_in(h):
        remote(sendl.at[0], recvl.at[h], l_s.at[0], l_r.at[h], c_peer).wait_recv()
        total = lower[...]
        for s in range(slots):
            total += nt_dot(recvl[h, s], tiles[h, s])
        lower[...] = total

    loop(0, me, lower_in)

    lower[...] += part[ry * nrz + rz]

    def from_z(i):
        z = z_other(i)
        remote(part.at[0], zrecv.at[z], z_s.at[0], z_r.at[z], c_peer).wait_recv()
        lower[...] += zrecv[z]

    loop(0, nrz - 1, from_z)
    prod_out[...] = lower[...]

    def gram_in(g):
        remote(gsend, grecv.at[g], g_s.at[0], g_r.at[g], c_peer).wait_recv()

    loop(0, me, gram_in)
    loop(me + 1, groups, gram_in)
    total = grecv[0]
    for g in range(1, groups):
        total += grecv[g]
    gram_out[...] = total

    def sent_down(h):
        table_send(h).wait_send()
        sums_send(h).wait_send()
        mirror_send(h).wait_send()
        gram_send(h).wait_send()

    def sent_up(g):
        lower_send(g).wait_send()
        gram_send(g).wait_send()

    loop(0, me, sent_down)
    loop(me + 1, groups, sent_up)

    def sent_z(i):
        z = z_other(i)
        z_send(z).wait_send()
        row_z_send(z).wait_send()

    loop(0, nrz - 1, sent_z)

    def sent_y(z):
        y_send(z, factor).wait_send()
        row_y_send(z).wait_send()

    loop(0, nrz, sent_y)

    def sent_c(j):
        c_send(j // nrz, j % nrz, factor).wait_send()
        core_send(j).wait_send()

    loop(0, nry * nrz, sent_c)


def exchange(sizes, blocks, columns, factor):
    _, groups, slots, tile, _ = blocks.shape
    rank = factor.shape[0]
    _, _, nry, nrz, nrc = sizes
    rows_grp = nry * nrz * nrc
    pairs = nry * nrz
    f32, bf16, i32, i16 = jnp.float32, jnp.bfloat16, jnp.int32, jnp.int16
    dma = pltpu.SemaphoreType.DMA
    one = (rank, tile)
    vmem = pl.BlockSpec(memory_space=pltpu.VMEM)
    return pl.pallas_call(
        functools.partial(exchange_kernel, sizes),
        out_shape=(jax.ShapeDtypeStruct(one, f32), jax.ShapeDtypeStruct((rank, LANES), f32)),
        in_specs=[pl.BlockSpec(memory_space=pl.ANY), vmem, vmem],
        out_specs=(vmem, vmem),
        scratch_shapes=[
            pltpu.VMEM((groups, slots, tile, tile), bf16),
            pltpu.VMEM((rows_grp + 1, *one), bf16),
            pltpu.VMEM((groups, 8, LANES), i32),
            pltpu.VMEM((groups, 8, LANES), i32),
            pltpu.SMEM((groups, 8, LANES), i32),
            pltpu.VMEM((8, LANES), f32),
            pltpu.VMEM((groups, 8, LANES), f32),
            pltpu.VMEM((groups, *one), f32),
            pltpu.VMEM(one, f32),
            pltpu.VMEM((groups, slots, *one), i16),
            pltpu.VMEM((groups, slots + 1, *one), i16),
            pltpu.VMEM((slots + 1, *one), f32),
            pltpu.VMEM((groups, slots, *one), bf16),
            pltpu.VMEM((groups, slots, *one), bf16),
            pltpu.VMEM(one, f32),
            pltpu.VMEM((rank, LANES), f32),
            pltpu.VMEM((groups, rank, LANES), f32),
            pltpu.VMEM((pairs, *one), f32),
            pltpu.VMEM((pairs, *one), f32),
            pltpu.VMEM((pairs, *one), f32),
            pltpu.VMEM((nrz, *one), f32),
            pltpu.VMEM((nrz, *one), f32),
            dma((groups,)),
            dma,
            dma((2 * nrz + pairs,)),
            dma((rows_grp,)),
            *[dma((groups,))] * 10,
            *[dma((pairs,))] * 2,
            *[dma((nrz,))] * 4,
        ],
        compiler_params=pltpu.CompilerParams(
            collective_id=0, has_side_effects=True, vmem_limit_bytes=48 * 1024 * 1024
        ),
        name="exchange",
    )(blocks, columns, factor)


def sweep_kernel(products, gram, factor, out):
    rank, tile = factor.shape
    current = factor[...].astype(jnp.float32)
    gram_all = gram[:, 0:rank]
    fitted = lax.dot_general(
        gram_all,
        current,
        (((0,), (0,)), ((), ())),
        precision=lax.Precision.HIGHEST,
        preferred_element_type=jnp.float32,
    )
    excess = products[...] - fitted
    place = lax.broadcasted_iota(jnp.int32, (rank, rank), 0)
    lane = lax.broadcasted_iota(jnp.int32, (rank, rank), 1)
    diagonal = jnp.sum(jnp.where(place == lane, gram_all, 0.0), axis=1, keepdims=True)
    inverse = 1.0 / diagonal
    for k in range(rank):
        first = k // 8 * 8
        at = k - first
        present = current[k : k + 1]
        fresh = jnp.maximum(present + excess[at : at + 1] * inverse[k : k + 1], floor_value)
        out[k : k + 1, :] = fresh
        if k + 1 < rank:
            change = fresh - present
            keep = 8 if at == 7 else 0
            excess = excess[keep:] - gram_all[first + keep :, k : k + 1] * change


def sweep(products, gram, factor):
    return pl.pallas_call(
        sweep_kernel,
        out_shape=jax.ShapeDtypeStruct(factor.shape, jnp.float32),
        name="sweep",
    )(products, gram, factor)


def solution(mesh):
    groups, rows_grp = mesh.shape["grp"], mesh.shape["row"]
    sizes = (groups // 2, 2, 2, rows_grp // 4, 2)
    split = Mesh(mesh.devices.reshape(sizes), AXES)

    def per_device(blocks, columns, factor):
        products, gram = exchange(sizes, blocks, columns, factor)
        return sweep(products, gram, factor)

    placed = (P(AXES, None, None, None, None), P(AXES, None, None), P(None, AXES))
    return jax.shard_map(
        per_device, mesh=split, in_specs=placed, out_specs=P(None, AXES), check_vma=False
    )
```

```python
import functools

import jax
import jax.numpy as jnp
from jax import lax
from jax.experimental import pallas as pl
from jax.experimental.pallas import tpu as pltpu
from jax.sharding import Mesh
from jax.sharding import PartitionSpec as P

AXES = ("grp_0", "grp_1", "row_0", "row_1", "row_2")
BY_MESH = pl.DeviceIdType.MESH
LANES = 128
INV_LANE = 32
CHUNKS = 4
LEVELS = 65534.0
OFFSET = 32768.0
floor_value = 1e-6


def nt_dot(a, b):
    return lax.dot_general(a, b, (((1,), (1,)), ((), ())), preferred_element_type=jnp.float32)


def to_column(row, rank):
    spread = jnp.broadcast_to(row, (rank, LANES))
    lane = lax.broadcasted_iota(jnp.int32, (rank, LANES), 1)
    place = lax.broadcasted_iota(jnp.int32, (rank, LANES), 0)
    return jnp.sum(jnp.where(lane == place, spread, 0.0), axis=1, keepdims=True)


def exchange_kernel(
    sizes,
    blocks,
    cols,
    factor,
    prod_out,
    gram_out,
    tiles,
    hall,
    tab,
    tabin,
    tabs,
    sums,
    sumsin,
    scale,
    base,
    sendm,
    recvm,
    ownm,
    sendl,
    recvl,
    lower,
    gsend,
    grecv,
    part,
    cbuf,
    crecv,
    yrecv,
    zrecv,
    blk_sem,
    tab_sem,
    ag_s,
    ag_r,
    tab_s,
    tab_r,
    sum_s,
    sum_r,
    m_s,
    m_r,
    l_s,
    l_r,
    g_s,
    g_r,
    c_s,
    c_r,
    y_s,
    y_r,
    z_s,
    z_r,
):
    _, ngy, nry, nrz, nrc = sizes
    gx, gy, ry, rz, rc = [lax.axis_index(axis) for axis in AXES]
    groups, slots = tiles.shape[0], tiles.shape[1]
    rank, tile = factor.shape
    rows_grp = nry * nrz * nrc
    me = gx * ngy + gy

    def place(y, z, c):
        return (y * nrz + z) * nrc + c

    mine = place(ry, rz, rc)
    deep = rank // CHUNKS
    half = nrz

    def group_peer(h):
        hx, hy = h // ngy, h % ngy
        flip = (hy - gy) * (hy - gy)
        return (hx, hy, ry + flip - 2 * ry * flip, rz, rc)

    def z_peer(z):
        return (gx, gy, ry, z, rc)

    y_peer = (gx, gy, 1 - ry, rz, rc)
    c_peer = (gx, gy, ry, rz, 1 - rc)

    def z_other(i):
        step = (i // 2 + 1) * (1 - 2 * (i % 2))
        return (rz + step + nrz) % nrz

    def remote(src, dst, send, recv, peer):
        return pltpu.make_async_remote_copy(
            src_ref=src, dst_ref=dst, send_sem=send, recv_sem=recv, device_id=peer, device_id_type=BY_MESH
        )

    def block_copy(h):
        return pltpu.make_async_copy(blocks.at[0, h], tiles.at[h], blk_sem.at[h])

    def loop(start, stop, body):
        def step(i, carry):
            body(i)
            return carry

        lax.fori_loop(start, stop, step, 0)

    loop(0, me + 1, lambda h: block_copy(h).start())

    hall[mine] = factor[...]
    hall[rows_grp] = jnp.zeros((rank, tile), hall.dtype)
    for g in range(groups):
        for c in range(CHUNKS):
            recvm[c][g, slots] = jnp.full((deep, tile), -32768, jnp.int32).astype(sendm.dtype)
    for c in range(CHUNKS):
        ownm[c, slots] = jnp.zeros((deep, tile), jnp.float32)
    all_cols = cols[0]
    lane = lax.broadcasted_iota(jnp.int32, (groups, LANES), 1)
    row = lax.broadcasted_iota(jnp.int32, (groups, LANES), 0)
    table = jnp.where(lane >= INV_LANE, slots, rows_grp)
    for s in range(slots):
        column = jnp.broadcast_to(all_cols[:, s : s + 1], (groups, LANES))
        offset = column - row * rows_grp
        live = (offset >= 0) & (offset < rows_grp)
        table = jnp.where(live & (lane == s), offset, table)
        table = jnp.where(live & (lane - INV_LANE == offset), s, table)
    for h in range(groups):
        tab[h] = jnp.broadcast_to(table[h : h + 1], (8, LANES))
        tabin[h] = jnp.zeros((8, LANES), jnp.int32)
    tabin[me] = tab[me]
    row_sums = nt_dot(jnp.ones((8, tile), jnp.bfloat16), factor[...])
    sums[...] = jnp.zeros((8, LANES), jnp.float32)
    sums[:, 0:rank] = jnp.maximum(row_sums, 1e-30)
    to_levels = LEVELS / to_column(sums[0:1, :], rank)

    barrier = pltpu.get_barrier_semaphore()

    def greet(peer):
        pl.semaphore_signal(barrier, inc=1, device_id=peer, device_id_type=BY_MESH)

    loop(0, me, lambda h: greet(group_peer(h)))
    loop(me + 1, groups, lambda h: greet(group_peer(h)))
    loop(0, nrz - 1, lambda i: greet(z_peer(z_other(i))))
    greet(y_peer)
    greet(c_peer)
    pl.semaphore_wait(barrier, groups - 1 + nrz - 1 + 2)

    def z_send(z):
        return remote(factor, hall.at[mine], ag_s.at[z], ag_r.at[mine], z_peer(z))

    def y_send(z, src):
        p = place(ry, z, rc)
        return remote(src, hall.at[p], ag_s.at[nrz + z], ag_r.at[p], y_peer)

    def c_send(y, z, src):
        p = place(y, z, rc)
        return remote(src, hall.at[p], ag_s.at[2 * nrz + y * nrz + z], ag_r.at[p], c_peer)

    def arrived(p):
        remote(factor, hall.at[p], ag_s.at[0], ag_r.at[p], c_peer).wait_recv()

    loop(0, nrz - 1, lambda i: z_send(z_other(i)).start())
    y_send(rz, factor).start()
    c_send(ry, rz, factor).start()

    def table_send(h):
        return remote(tab.at[h], tabin.at[me], tab_s.at[h], tab_r.at[me], group_peer(h))

    def sums_send(h):
        return remote(sums, sumsin.at[me], sum_s.at[h], sum_r.at[me], group_peer(h))

    def small_sends(h):
        table_send(h).start()
        sums_send(h).start()

    loop(0, me, small_sends)

    def mirror_send(h, c):
        return remote(
            sendm.at[h, c], recvm[c].at[me, pl.ds(0, slots)], m_s.at[h, c], m_r.at[me, c], group_peer(h)
        )

    def mirror(h):
        block_copy(h).wait()
        for s in range(slots):
            product = jnp.dot(factor[...], tiles[h, s], preferred_element_type=jnp.float32)
            coded = jnp.round(product * to_levels - OFFSET).astype(jnp.int32).astype(sendm.dtype)
            for c in range(CHUNKS):
                sendm[h, c, s] = coded[c * deep : (c + 1) * deep]
        mirror_send(h, 0).start()

    loop(0, me, mirror)
    for chunk in range(1, CHUNKS):
        loop(0, me, lambda h: mirror_send(h, chunk).start())

    def forward(i):
        z = z_other(i)
        p = place(ry, z, rc)
        arrived(p)
        y_send(z, hall.at[p]).start()
        c_send(ry, z, hall.at[p]).start()

    loop(0, nrz - 1, forward)

    def second_step(i):
        z = (rz + i) % nrz
        p = place(1 - ry, z, rc)
        arrived(p)
        c_send(1 - ry, z, hall.at[p]).start()

    loop(0, nrz, second_step)

    def tables_in(g):
        remote(tab.at[0], tabin.at[g], tab_s.at[0], tab_r.at[g], c_peer).wait_recv()
        remote(sums, sumsin.at[g], sum_s.at[0], sum_r.at[g], c_peer).wait_recv()
        column = to_column(sumsin[g][0:1, :], rank) * (1.0 / LEVELS)
        scale[g] = jnp.broadcast_to(column, (rank, tile))

    loop(me + 1, groups, tables_in)
    to_scalars = pltpu.make_async_copy(tabin, tabs, tab_sem)
    to_scalars.start()
    to_scalars.wait()
    loop(0, nry * nrz, lambda j: arrived(j * nrc + 1 - rc))

    def lower_send(g):
        return remote(sendl.at[g], recvl.at[me], l_s.at[g], l_r.at[me], group_peer(g))

    def serve(g):
        for s in range(slots):
            sendl[g, s] = hall[tabs[g, 0, s]]
        lower_send(g).start()

    loop(me + 1, groups, serve)

    def gram_step(p, total):
        return total + nt_dot(hall[p], hall[p])

    group_gram = lax.fori_loop(0, rows_grp, gram_step, jnp.zeros((rank, rank), jnp.float32))
    gsend[...] = jnp.zeros((rank, LANES), jnp.float32)
    gsend[:, 0:rank] = group_gram
    grecv[me] = gsend[...]

    block_copy(me).wait()
    lower[...] = jnp.zeros((rank, tile), jnp.float32)
    for s in range(slots):
        product = jnp.dot(factor[...], tiles[me, s], preferred_element_type=jnp.float32)
        for c in range(CHUNKS):
            ownm[c, s] = product[c * deep : (c + 1) * deep]
        lower[...] += nt_dot(hall[tabs[me, 0, s]], tiles[me, s])

    def gram_send(h):
        return remote(gsend, grecv.at[me], g_s.at[h], g_r.at[me], group_peer(h))

    loop(0, me, lambda h: gram_send(h).start())
    loop(me + 1, groups, lambda h: gram_send(h).start())

    base[...] = jnp.zeros((rank, tile), jnp.float32)

    def add_offset(g):
        base[...] += OFFSET * scale[g]

    loop(me + 1, groups, add_offset)
    other, own = (1 - ry) * nrz, ry * nrz

    def core_send(c, y):
        first = pl.ds(y * nrz, half)
        return remote(cbuf.at[c, first], crecv.at[c, first], c_s.at[c, y], c_r.at[c, y], c_peer)

    def row_y_send(c):
        return remote(part.at[c, pl.ds(other, half)], yrecv.at[c], y_s.at[c], y_r.at[c], y_peer)

    def row_z_send(c, z):
        return remote(part.at[c, own + z], zrecv.at[c, rz], z_s.at[c, z], z_r.at[c, rz], z_peer(z))

    def sum_chunk(c):
        rows = slice(c * deep, (c + 1) * deep)

        def mirror_in(g):
            remote(
                sendm.at[0, c], recvm[c].at[g, pl.ds(0, slots)], m_s.at[0, c], m_r.at[g, c], c_peer
            ).wait_recv()

        loop(me + 1, groups, mirror_in)

        def summed(p):
            def add(g, total):
                coded = recvm[c][g, tabs[g, 0, INV_LANE + p]].astype(jnp.int32).astype(jnp.float32)
                return total + coded * scale[g, rows, :]

            start = base[rows, :] + ownm[c, tabs[me, 0, INV_LANE + p]]
            return lax.fori_loop(me + 1, groups, add, start)

        def for_other_core(j):
            cbuf[c, j] = summed(j * nrc + 1 - rc)

        def for_this_core(j):
            part[c, j] = summed(j * nrc + rc)

        loop(other, other + half, for_other_core)
        core_send(c, 1 - ry).start()
        loop(own, own + half, for_other_core)
        core_send(c, ry).start()
        loop(0, nry * nrz, for_this_core)

    def chunk_to_y(c):
        core_send(c, 1 - ry).wait_recv()

        def add(j):
            part[c, j] += crecv[c, j]

        loop(other, other + half, add)
        row_y_send(c).start()

    def chunk_to_z(c):
        core_send(c, ry).wait_recv()
        row_y_send(c).wait_recv()

        def add(z):
            part[c, own + z] += crecv[c, own + z] + yrecv[c, z]

        def send(i):
            row_z_send(c, z_other(i)).start()

        loop(0, nrz, add)
        loop(0, nrz - 1, send)

    for chunk in range(CHUNKS):
        sum_chunk(chunk)
        if chunk > 0:
            chunk_to_z(chunk - 1)
        chunk_to_y(chunk)
    chunk_to_z(CHUNKS - 1)

    def lower_in(h):
        remote(sendl.at[0], recvl.at[h], l_s.at[0], l_r.at[h], c_peer).wait_recv()
        total = lower[...]
        for s in range(slots):
            total += nt_dot(recvl[h, s], tiles[h, s])
        lower[...] = total

    loop(0, me, lower_in)

    for chunk in range(CHUNKS):
        rows = slice(chunk * deep, (chunk + 1) * deep)
        lower[rows, :] += part[chunk, own + rz]

        def from_z(i):
            z = z_other(i)
            remote(
                part.at[chunk, 0], zrecv.at[chunk, z], z_s.at[chunk, 0], z_r.at[chunk, z], c_peer
            ).wait_recv()
            lower[rows, :] += zrecv[chunk, z]

        loop(0, nrz - 1, from_z)
    prod_out[...] = lower[...]

    def gram_in(g):
        remote(gsend, grecv.at[g], g_s.at[0], g_r.at[g], c_peer).wait_recv()

    loop(0, me, gram_in)
    loop(me + 1, groups, gram_in)
    total = grecv[0]
    for g in range(1, groups):
        total += grecv[g]
    gram_out[...] = total

    def sent_down(h):
        table_send(h).wait_send()
        sums_send(h).wait_send()
        for c in range(CHUNKS):
            mirror_send(h, c).wait_send()
        gram_send(h).wait_send()

    def sent_up(g):
        lower_send(g).wait_send()
        gram_send(g).wait_send()

    loop(0, me, sent_down)
    loop(me + 1, groups, sent_up)

    def sent_z(i):
        z = z_other(i)
        z_send(z).wait_send()
        for c in range(CHUNKS):
            row_z_send(c, z).wait_send()

    loop(0, nrz - 1, sent_z)

    def sent_y(z):
        y_send(z, factor).wait_send()

    loop(0, nrz, sent_y)

    def sent_c(j):
        c_send(j // nrz, j % nrz, factor).wait_send()
    loop(0, nry * nrz, sent_c)
    for c in range(CHUNKS):
        row_y_send(c).wait_send()
        for y in range(nry):
            core_send(c, y).wait_send()


def exchange(sizes, blocks, columns, factor):
    _, groups, slots, tile, _ = blocks.shape
    rank = factor.shape[0]
    _, _, nry, nrz, nrc = sizes
    rows_grp = nry * nrz * nrc
    pairs = nry * nrz
    f32, bf16, i32, i16 = jnp.float32, jnp.bfloat16, jnp.int32, jnp.int16
    dma = pltpu.SemaphoreType.DMA
    one = (rank, tile)
    deep = (rank // CHUNKS, tile)
    vmem = pl.BlockSpec(memory_space=pltpu.VMEM)
    return pl.pallas_call(
        functools.partial(exchange_kernel, sizes),
        out_shape=(jax.ShapeDtypeStruct(one, f32), jax.ShapeDtypeStruct((rank, LANES), f32)),
        in_specs=[pl.BlockSpec(memory_space=pl.ANY), vmem, vmem],
        out_specs=(vmem, vmem),
        scratch_shapes=[
            pltpu.VMEM((groups, slots, tile, tile), bf16),
            pltpu.VMEM((rows_grp + 1, *one), bf16),
            pltpu.VMEM((groups, 8, LANES), i32),
            pltpu.VMEM((groups, 8, LANES), i32),
            pltpu.SMEM((groups, 8, LANES), i32),
            pltpu.VMEM((8, LANES), f32),
            pltpu.VMEM((groups, 8, LANES), f32),
            pltpu.VMEM((groups, *one), f32),
            pltpu.VMEM(one, f32),
            pltpu.VMEM((groups, CHUNKS, slots, *deep), i16),
            [pltpu.VMEM((groups, slots + 1, *deep), i16)] * CHUNKS,
            pltpu.VMEM((CHUNKS, slots + 1, *deep), f32),
            pltpu.VMEM((groups, slots, *one), bf16),
            pltpu.VMEM((groups, slots, *one), bf16),
            pltpu.VMEM(one, f32),
            pltpu.VMEM((rank, LANES), f32),
            pltpu.VMEM((groups, rank, LANES), f32),
            pltpu.VMEM((CHUNKS, pairs, *deep), f32),
            pltpu.VMEM((CHUNKS, pairs, *deep), f32),
            pltpu.VMEM((CHUNKS, pairs, *deep), f32),
            pltpu.VMEM((CHUNKS, nrz, *deep), f32),
            pltpu.VMEM((CHUNKS, nrz, *deep), f32),
            dma((groups,)),
            dma,
            dma((2 * nrz + pairs,)),
            dma((rows_grp,)),
            *[dma((groups,))] * 4,
            *[dma((groups, CHUNKS))] * 2,
            *[dma((groups,))] * 4,
            *[dma((CHUNKS, nry))] * 2,
            *[dma((CHUNKS,))] * 2,
            *[dma((CHUNKS, nrz))] * 2,
        ],
        compiler_params=pltpu.CompilerParams(
            collective_id=0, has_side_effects=True, vmem_limit_bytes=48 * 1024 * 1024
        ),
        name="exchange",
    )(blocks, columns, factor)


def sweep_kernel(products, gram, factor, out):
    rank, tile = factor.shape
    current = factor[...].astype(jnp.float32)
    gram_all = gram[:, 0:rank]
    fitted = lax.dot_general(
        gram_all,
        current,
        (((0,), (0,)), ((), ())),
        precision=lax.Precision.HIGHEST,
        preferred_element_type=jnp.float32,
    )
    excess = products[...] - fitted
    place = lax.broadcasted_iota(jnp.int32, (rank, rank), 0)
    lane = lax.broadcasted_iota(jnp.int32, (rank, rank), 1)
    diagonal = jnp.sum(jnp.where(place == lane, gram_all, 0.0), axis=1, keepdims=True)
    inverse = 1.0 / diagonal
    for k in range(rank):
        first = k // 8 * 8
        at = k - first
        present = current[k : k + 1]
        fresh = jnp.maximum(present + excess[at : at + 1] * inverse[k : k + 1], floor_value)
        out[k : k + 1, :] = fresh
        if k + 1 < rank:
            change = fresh - present
            keep = 8 if at == 7 else 0
            excess = excess[keep:] - gram_all[first + keep :, k : k + 1] * change


def sweep(products, gram, factor):
    return pl.pallas_call(
        sweep_kernel,
        out_shape=jax.ShapeDtypeStruct(factor.shape, jnp.float32),
        name="sweep",
    )(products, gram, factor)


def solution(mesh):
    groups, rows_grp = mesh.shape["grp"], mesh.shape["row"]
    sizes = (groups // 2, 2, 2, rows_grp // 4, 2)
    split = Mesh(mesh.devices.reshape(sizes), AXES)

    def per_device(blocks, columns, factor):
        products, gram = exchange(sizes, blocks, columns, factor)
        return sweep(products, gram, factor)

    placed = (P(AXES, None, None, None, None), P(AXES, None, None), P(None, AXES))
    return jax.shard_map(
        per_device, mesh=split, in_specs=placed, out_specs=P(None, AXES), check_vma=False
    )
```

```python
import functools

import jax
import jax.numpy as jnp
from jax import lax
from jax.experimental import pallas as pl
from jax.experimental.pallas import tpu as pltpu
from jax.sharding import Mesh
from jax.sharding import PartitionSpec as P

AXES = ("grp_0", "grp_1", "row_0", "row_1", "row_2")
BY_MESH = pl.DeviceIdType.MESH
LANES = 128
INV_LANE = 32
CHUNKS = 4
LEVELS = 65534.0
OFFSET = 32768.0
floor_value = 1e-6


def nt_dot(a, b):
    return lax.dot_general(a, b, (((1,), (1,)), ((), ())), preferred_element_type=jnp.float32)


def to_column(row, rank):
    spread = jnp.broadcast_to(row, (rank, LANES))
    lane = lax.broadcasted_iota(jnp.int32, (rank, LANES), 1)
    place = lax.broadcasted_iota(jnp.int32, (rank, LANES), 0)
    return jnp.sum(jnp.where(lane == place, spread, 0.0), axis=1, keepdims=True)


def exchange_kernel(
    sizes,
    blocks,
    cols_in,
    factor_in,
    out,
    cols,
    factor,
    tiles,
    hall,
    hfar,
    tab,
    tabin,
    tabs,
    sums,
    sumsin,
    scale,
    base,
    sendm,
    recvm,
    ownm,
    sendl,
    recvl,
    lower,
    gsend,
    grecv,
    part,
    cbuf,
    crecv,
    yrecv,
    zrecv,
    in_sem,
    blk_sem,
    tab_sem,
    ag_s,
    ag_r,
    far_s,
    far_r,
    seed_s,
    tab_s,
    tab_r,
    sum_s,
    sum_r,
    m_s,
    m_r,
    l_s,
    l_r,
    g_s,
    g_r,
    c_s,
    c_r,
    y_s,
    y_r,
    z_s,
    z_r,
):
    ngx, ngy, nry, nrz, nrc = sizes
    gx, gy, ry, rz, rc = [lax.axis_index(axis) for axis in AXES]
    groups, slots = tiles.shape[0], tiles.shape[1]
    rank, tile = factor.shape
    rows_grp = nry * nrz * nrc
    me = gx * ngy + gy
    far = ngx // 2

    def place(y, z, c):
        return (y * nrz + z) * nrc + c

    mine = place(ry, rz, rc)
    deep = rank // CHUNKS
    half = nrz

    def group_peer(h):
        hx, hy = h // ngy, h % ngy
        flip = (hy - gy) * (hy - gy)
        return (hx, hy, ry + flip - 2 * ry * flip, rz, rc)

    def z_peer(z):
        return (gx, gy, ry, z, rc)

    y_peer = (gx, gy, 1 - ry, rz, rc)
    c_peer = (gx, gy, ry, rz, 1 - rc)

    def z_other(i):
        step = (i // 2 + 1) * (1 - 2 * (i % 2))
        return (rz + step + nrz) % nrz

    def remote(src, dst, send, recv, peer):
        return pltpu.make_async_remote_copy(
            src_ref=src, dst_ref=dst, send_sem=send, recv_sem=recv, device_id=peer, device_id_type=BY_MESH
        )

    def block_copy(h):
        return pltpu.make_async_copy(blocks.at[0, h], tiles.at[h], blk_sem.at[h])

    def loop(start, stop, body):
        def step(i, carry):
            body(i)
            return carry

        lax.fori_loop(start, stop, step, 0)

    cols_copy = pltpu.make_async_copy(cols_in, cols, in_sem.at[0])
    factor_copy = pltpu.make_async_copy(factor_in, factor, in_sem.at[1])
    cols_copy.start()
    factor_copy.start()
    barrier = pltpu.get_barrier_semaphore()

    def greet(peer):
        pl.semaphore_signal(barrier, inc=1, device_id=peer, device_id_type=BY_MESH)

    loop(0, me, lambda h: greet(group_peer(h)))
    loop(me + 1, groups, lambda h: greet(group_peer(h)))
    loop(0, nrz - 1, lambda i: greet(z_peer(z_other(i))))
    greet(y_peer)
    greet(c_peer)
    loop(0, me + 1, lambda h: block_copy(h).start())

    hall[rows_grp] = jnp.zeros((rank, tile), hall.dtype)
    for q in range(ngy):
        hfar[q, rows_grp] = jnp.zeros((rank, tile), hall.dtype)
    for g in range(groups):
        for c in range(CHUNKS):
            recvm[c][g, slots] = jnp.full((deep, tile), -32768, jnp.int32).astype(sendm.dtype)
    for c in range(CHUNKS):
        ownm[c, slots] = jnp.zeros((deep, tile), jnp.float32)
    cols_copy.wait()
    factor_copy.wait()
    hall[mine] = factor[...]
    all_cols = cols[0]
    lane = lax.broadcasted_iota(jnp.int32, (groups, LANES), 1)
    row = lax.broadcasted_iota(jnp.int32, (groups, LANES), 0)
    table = jnp.where(lane >= INV_LANE, slots, rows_grp)
    for s in range(slots):
        column = jnp.broadcast_to(all_cols[:, s : s + 1], (groups, LANES))
        offset = column - row * rows_grp
        live = (offset >= 0) & (offset < rows_grp)
        table = jnp.where(live & (lane == s), offset, table)
        table = jnp.where(live & (lane - INV_LANE == offset), s, table)
    for h in range(groups):
        tab[h] = jnp.broadcast_to(table[h : h + 1], (8, LANES))

    def keep_own(h):
        tabin[h] = tab[h]

    loop(0, me + 1, keep_own)
    row_sums = nt_dot(jnp.ones((8, tile), jnp.bfloat16), factor[...])
    sums[...] = jnp.zeros((8, LANES), jnp.float32)
    sums[:, 0:rank] = jnp.maximum(row_sums, 1e-30)
    to_levels = LEVELS / to_column(sums[0:1, :], rank)

    def mirror_send(h, c):
        return remote(
            sendm.at[h, c], recvm[c].at[me, pl.ds(0, slots)], m_s.at[h, c], m_r.at[me, c], group_peer(h)
        )

    def mirror(h):
        block_copy(h).wait()
        for s in range(slots):
            product = jnp.dot(factor[...], tiles[h, s], preferred_element_type=jnp.float32)
            coded = jnp.round(product * to_levels - OFFSET).astype(jnp.int32).astype(sendm.dtype)
            for c in range(CHUNKS):
                sendm[h, c, s] = coded[c * deep : (c + 1) * deep]

    pl.semaphore_wait(barrier, groups - 1 + nrz - 1 + 2)

    class Gather:
        def __init__(self, held, send, recv, y):
            self.held, self.send, self.recv, self.y = held, send, recv, y
            self.seed = place(y, rz, rc)

        def z_copy(self, z, src):
            p = self.seed
            return remote(src, self.held.at[p], self.send.at[z], self.recv.at[p], z_peer(z))

        def y_copy(self, z, src):
            p = place(self.y, z, rc)
            return remote(src, self.held.at[p], self.send.at[nrz + z], self.recv.at[p], y_peer)

        def c_copy(self, y, z, src):
            p = place(y, z, rc)
            return remote(src, self.held.at[p], self.send.at[(2 + y) * nrz + z], self.recv.at[p], c_peer)

        def arrived(self, p):
            remote(factor, self.held.at[p], self.send.at[0], self.recv.at[p], c_peer).wait_recv()

        def begin(self, src):
            loop(0, nrz - 1, lambda i: self.z_copy(z_other(i), src).start())
            self.y_copy(rz, src).start()
            self.c_copy(self.y, rz, src).start()

        def forward(self, i):
            z = z_other(i)
            p = place(self.y, z, rc)
            self.arrived(p)
            self.y_copy(z, self.held.at[p]).start()
            self.c_copy(self.y, z, self.held.at[p]).start()

        def second(self, i):
            z = (rz + i) % nrz
            p = place(1 - self.y, z, rc)
            self.arrived(p)
            self.c_copy(1 - self.y, z, self.held.at[p]).start()

        def finish(self):
            loop(0, nry * nrz, lambda j: self.arrived(j * nrc + 1 - rc))

        def drain(self):
            loop(0, nrz - 1, lambda i: self.z_copy(z_other(i), factor).wait_send())
            loop(0, nrz, lambda z: self.y_copy(z, factor).wait_send())
            loop(0, nry * nrz, lambda j: self.c_copy(j // nrz, j % nrz, factor).wait_send())

    def flipped(y, q):
        flip = (q - gy) * (q - gy)
        return y + flip - 2 * y * flip

    near_set = Gather(hall, ag_s, ag_r, ry)
    far_sets = [Gather(hfar.at[q], far_s.at[q], far_r.at[q], flipped(ry, q)) for q in range(ngy)]

    def seed_send(q):
        peer = (gx + far, q, flipped(ry, q), rz, rc)
        return remote(factor, hfar.at[gy, mine], seed_s.at[q], far_r.at[gy, mine], peer)

    def when_far(body):
        pl.when(gx >= far)(body)

    near_set.begin(factor)

    @pl.when(gx < far)
    def _():
        for q in range(ngy):
            seed_send(q).start()

    def table_send(h):
        return remote(tab.at[h], tabin.at[me], tab_s.at[h], tab_r.at[me], group_peer(h))

    def sums_send(h):
        return remote(sums, sumsin.at[me], sum_s.at[h], sum_r.at[me], group_peer(h))

    def small_sends(h):
        table_send(h).start()
        sums_send(h).start()

    loop(0, me, small_sends)

    def mirror_late(h):
        mirror(h)
        mirror_send(h, 0).start()

    loop(0, me, mirror_late)
    for chunk in range(1, CHUNKS):
        loop(0, me, lambda h: mirror_send(h, chunk).start())

    block_copy(me).wait()
    for s in range(slots):
        product = jnp.dot(factor[...], tiles[me, s], preferred_element_type=jnp.float32)
        for c in range(CHUNKS):
            ownm[c, s] = product[c * deep : (c + 1) * deep]

    loop(0, nrz - 1, near_set.forward)

    @when_far
    def _():
        for held in far_sets:
            held.arrived(held.seed)
            held.begin(held.held.at[held.seed])

    loop(0, nrz, near_set.second)

    def tables_in(g):
        remote(tab.at[0], tabin.at[g], tab_s.at[0], tab_r.at[g], c_peer).wait_recv()
        remote(sums, sumsin.at[g], sum_s.at[0], sum_r.at[g], c_peer).wait_recv()
        column = to_column(sumsin[g][0:1, :], rank) * (1.0 / LEVELS)
        scale[g] = jnp.broadcast_to(column, (rank, tile))

    loop(me + 1, groups, tables_in)
    to_scalars = pltpu.make_async_copy(tabin, tabs, tab_sem)
    to_scalars.start()
    to_scalars.wait()
    near_set.finish()

    def lower_send(g):
        return remote(sendl.at[g], recvl.at[me], l_s.at[g], l_r.at[me], group_peer(g))

    def serve(g):
        @pl.when(g // ngy != gx + far)
        def _():
            for s in range(slots):
                sendl[g, s] = hall[tabs[g, 0, s]]
            lower_send(g).start()

    loop(me + 1, groups, serve)

    gsend[...] = jnp.zeros((rank, LANES), jnp.float32)

    def gram_part(part_of):
        def step(i, total):
            for p in range(4):
                held = hall[part_of * (rows_grp // 2) + i * 4 + p]
                total += nt_dot(held, held)
            return total

        gsend[:, 0:rank] = lax.fori_loop(0, rows_grp // 8, step, gsend[:, 0:rank])

    def gram_send(h):
        return remote(gsend, grecv.at[me], g_s.at[h], g_r.at[me], group_peer(h))

    def gram_sends():
        grecv[me] = gsend[...]
        loop(0, me, lambda h: gram_send(h).start())
        loop(me + 1, groups, lambda h: gram_send(h).start())

    base[...] = jnp.zeros((rank, tile), jnp.float32)

    def no_scale(g):
        scale[g] = jnp.zeros((rank, tile), jnp.float32)

    loop(0, me + 1, no_scale)
    for g in range(1, groups):
        base[...] += OFFSET * scale[g]
    other, own = (1 - ry) * nrz, ry * nrz

    def core_send(c, y):
        first = pl.ds(y * nrz, half)
        return remote(cbuf.at[c, first], crecv.at[c, first], c_s.at[c, y], c_r.at[c, y], c_peer)

    def row_y_send(c):
        return remote(part.at[c, pl.ds(other, half)], yrecv.at[c], y_s.at[c], y_r.at[c], y_peer)

    def row_z_send(c, z):
        return remote(part.at[c, own + z], zrecv.at[c, rz], z_s.at[c, z], z_r.at[c, rz], z_peer(z))

    def sum_chunk(c):
        rows = slice(c * deep, (c + 1) * deep)

        def mirror_in(g):
            remote(
                sendm.at[0, c], recvm[c].at[g, pl.ds(0, slots)], m_s.at[0, c], m_r.at[g, c], c_peer
            ).wait_recv()

        loop(me + 1, groups, mirror_in)

        def summed(p):
            total = base[rows, :] + ownm[c, tabs[me, 0, INV_LANE + p]]
            for g in range(1, groups):
                slot = jnp.where(g > me, tabs[g, 0, INV_LANE + p], slots)
                total += recvm[c][g, slot].astype(jnp.int32).astype(jnp.float32) * scale[g, rows, :]
            return total

        def for_other_core(j):
            cbuf[c, j] = summed(j * nrc + 1 - rc)

        def for_this_core(j):
            part[c, j] = summed(j * nrc + rc)

        loop(other, other + half, for_other_core)
        core_send(c, 1 - ry).start()
        loop(own, own + half, for_other_core)
        core_send(c, ry).start()
        loop(0, nry * nrz, for_this_core)

    def chunk_to_y(c):
        core_send(c, 1 - ry).wait_recv()

        def add(j):
            part[c, j] += crecv[c, j]

        loop(other, other + half, add)
        row_y_send(c).start()

    def chunk_to_z(c):
        core_send(c, ry).wait_recv()
        row_y_send(c).wait_recv()

        def add(z):
            part[c, own + z] += crecv[c, own + z] + yrecv[c, z]

        def send(i):
            row_z_send(c, z_other(i)).start()

        loop(0, nrz, add)
        loop(0, nrz - 1, send)

    gram_part(0)
    gram_part(1)
    gram_sends()
    for c in range(CHUNKS):
        sum_chunk(c)
        if 1 <= c <= ngy:
            when_far(lambda: loop(0, nrz - 1, far_sets[c - 1].forward))
        if c > 0:
            chunk_to_z(c - 1)
        chunk_to_y(c)
    when_far(lambda: loop(0, nrz, far_sets[0].second))
    chunk_to_z(CHUNKS - 1)
    when_far(lambda: loop(0, nrz, far_sets[1].second))

    def lower_add(h, tile_of):
        total = lower[...]
        for s in range(slots):
            total += nt_dot(tile_of(s), tiles[h, s])
        lower[...] = total

    lower[...] = jnp.zeros((rank, tile), jnp.float32)
    lower_add(me, lambda s: hall[tabs[me, 0, s]])

    @when_far
    def _():
        for held in far_sets:
            held.finish()
        for q in range(ngy):
            h = (gx - far) * ngy + q
            lower_add(h, lambda s: hfar[q, tabs[h, 0, s]])

    def lower_in(h):
        @pl.when(h // ngy != gx - far)
        def _():
            remote(sendl.at[0], recvl.at[h], l_s.at[0], l_r.at[h], c_peer).wait_recv()
            lower_add(h, lambda s: recvl[h, s])

    loop(0, me, lower_in)

    def gram_in(g):
        remote(gsend, grecv.at[g], g_s.at[0], g_r.at[g], c_peer).wait_recv()

    loop(0, me, gram_in)
    loop(me + 1, groups, gram_in)
    total = grecv[0]
    for g in range(1, groups):
        total += grecv[g]
    gram = total[:, 0:rank]

    current = factor[...].astype(jnp.float32)
    fitted = lax.dot_general(
        gram,
        current,
        (((0,), (0,)), ((), ())),
        precision=lax.Precision.HIGHEST,
        preferred_element_type=jnp.float32,
    )
    excess = lower[...] - fitted
    across = lax.broadcasted_iota(jnp.int32, (rank, rank), 1)
    down = lax.broadcasted_iota(jnp.int32, (rank, rank), 0)
    inverse = 1.0 / jnp.sum(jnp.where(across == down, gram, 0.0), axis=1, keepdims=True)
    for chunk in range(CHUNKS):

        def from_z(i):
            z = z_other(i)
            remote(
                part.at[chunk, 0], zrecv.at[chunk, z], z_s.at[chunk, 0], z_r.at[chunk, z], c_peer
            ).wait_recv()
            part[chunk, own + rz] += zrecv[chunk, z]

        loop(0, nrz - 1, from_z)
        begin = chunk * deep % 8
        end = begin + deep
        pieces = [excess[:begin], excess[begin:end] + part[chunk, own + rz], excess[end:]]
        excess = jnp.concatenate([piece for piece in pieces if piece.shape[0]], axis=0)
        for k in range(chunk * deep, (chunk + 1) * deep):
            at = k % 8
            present = current[k : k + 1]
            fresh = jnp.maximum(present + excess[at : at + 1] * inverse[k : k + 1], floor_value)
            out[k : k + 1, :] = fresh
            if k + 1 < rank:
                keep = 8 if at == 7 else 0
                change = fresh - present
                excess = excess[keep:] - gram[k - at + keep :, k : k + 1] * change

    def sent_down(h):
        table_send(h).wait_send()
        sums_send(h).wait_send()
        for c in range(CHUNKS):
            mirror_send(h, c).wait_send()
        gram_send(h).wait_send()

    def sent_up(g):
        gram_send(g).wait_send()

        @pl.when(g // ngy != gx + far)
        def _():
            lower_send(g).wait_send()

    loop(0, me, sent_down)
    loop(me + 1, groups, sent_up)

    def sent_z(i):
        for c in range(CHUNKS):
            row_z_send(c, z_other(i)).wait_send()

    loop(0, nrz - 1, sent_z)
    near_set.drain()

    @pl.when(gx < far)
    def _():
        for q in range(ngy):
            seed_send(q).wait_send()

    @when_far
    def _():
        for held in far_sets:
            held.drain()

    for c in range(CHUNKS):
        row_y_send(c).wait_send()
        for y in range(nry):
            core_send(c, y).wait_send()


def exchange(sizes, blocks, columns, factor):
    _, groups, slots, tile, _ = blocks.shape
    rank = factor.shape[0]
    _, ngy, nry, nrz, nrc = sizes
    rows_grp = nry * nrz * nrc
    pairs = nry * nrz
    f32, bf16, i32, i16 = jnp.float32, jnp.bfloat16, jnp.int32, jnp.int16
    dma = pltpu.SemaphoreType.DMA
    one = (rank, tile)
    deep = (rank // CHUNKS, tile)
    vmem = pl.BlockSpec(memory_space=pltpu.VMEM)
    return pl.pallas_call(
        functools.partial(exchange_kernel, sizes),
        out_shape=jax.ShapeDtypeStruct(one, f32),
        in_specs=[pl.BlockSpec(memory_space=pl.ANY)] * 3,
        out_specs=vmem,
        scratch_shapes=[
            pltpu.VMEM(columns.shape, i32),
            pltpu.VMEM(one, bf16),
            pltpu.VMEM((groups, slots, tile, tile), bf16),
            pltpu.VMEM((rows_grp + 1, *one), bf16),
            pltpu.VMEM((ngy, rows_grp + 1, *one), bf16),
            pltpu.VMEM((groups, 8, LANES), i32),
            pltpu.VMEM((groups, 8, LANES), i32),
            pltpu.SMEM((groups, 8, LANES), i32),
            pltpu.VMEM((8, LANES), f32),
            pltpu.VMEM((groups, 8, LANES), f32),
            pltpu.VMEM((groups, *one), f32),
            pltpu.VMEM(one, f32),
            pltpu.VMEM((groups, CHUNKS, slots, *deep), i16),
            [pltpu.VMEM((groups, slots + 1, *deep), i16)] * CHUNKS,
            pltpu.VMEM((CHUNKS, slots + 1, *deep), f32),
            pltpu.VMEM((groups, slots, *one), bf16),
            pltpu.VMEM((groups, slots, *one), bf16),
            pltpu.VMEM(one, f32),
            pltpu.VMEM((rank, LANES), f32),
            pltpu.VMEM((groups, rank, LANES), f32),
            pltpu.VMEM((CHUNKS, pairs, *deep), f32),
            pltpu.VMEM((CHUNKS, pairs, *deep), f32),
            pltpu.VMEM((CHUNKS, pairs, *deep), f32),
            pltpu.VMEM((CHUNKS, nrz, *deep), f32),
            pltpu.VMEM((CHUNKS, nrz, *deep), f32),
            dma((2,)),
            dma((groups,)),
            dma,
            dma((2 * nrz + pairs,)),
            dma((rows_grp,)),
            dma((ngy, 2 * nrz + pairs)),
            dma((ngy, rows_grp)),
            dma((ngy,)),
            *[dma((groups,))] * 4,
            *[dma((groups, CHUNKS))] * 2,
            *[dma((groups,))] * 4,
            *[dma((CHUNKS, nry))] * 2,
            *[dma((CHUNKS,))] * 2,
            *[dma((CHUNKS, nrz))] * 2,
        ],
        compiler_params=pltpu.CompilerParams(
            collective_id=0, has_side_effects=True, vmem_limit_bytes=48 * 1024 * 1024
        ),
        name="exchange",
    )(blocks, columns, factor)


def solution(mesh):
    groups, rows_grp = mesh.shape["grp"], mesh.shape["row"]
    sizes = (groups // 2, 2, 2, rows_grp // 4, 2)
    split = Mesh(mesh.devices.reshape(sizes), AXES)

    def per_device(blocks, columns, factor):
        return exchange(sizes, blocks, columns, factor)

    placed = (P(AXES, None, None, None, None), P(AXES, None, None), P(None, AXES))
    return jax.shard_map(
        per_device, mesh=split, in_specs=placed, out_specs=P(None, AXES), check_vma=False
    )
```

```python
import functools

import jax
import jax.numpy as jnp
from jax import lax
from jax.experimental import pallas as pl
from jax.experimental.pallas import tpu as pltpu
from jax.sharding import Mesh
from jax.sharding import PartitionSpec as P

AXES = ("grp_0", "grp_1", "row_0", "row_1", "row_2")
BY_MESH = pl.DeviceIdType.MESH
LANES = 128
INV_LANE = 32
CHUNKS = 4
LEVELS = 65534.0
OFFSET = 32768.0
floor_value = 1e-6


def nt_dot(a, b):
    return lax.dot_general(a, b, (((1,), (1,)), ((), ())), preferred_element_type=jnp.float32)


def to_column(row, rank):
    spread = jnp.broadcast_to(row, (rank, LANES))
    lane = lax.broadcasted_iota(jnp.int32, (rank, LANES), 1)
    place = lax.broadcasted_iota(jnp.int32, (rank, LANES), 0)
    return jnp.sum(jnp.where(lane == place, spread, 0.0), axis=1, keepdims=True)


def exchange_kernel(
    sizes,
    blocks,
    cols_in,
    factor_in,
    out,
    cols,
    factor,
    tiles,
    hall,
    hfar,
    tab,
    tabin,
    tabs,
    sums,
    sumsin,
    scale,
    base,
    sendm,
    recvm,
    ownm,
    sendl,
    recvl,
    lower,
    gsend,
    grecv,
    part,
    cbuf,
    crecv,
    yrecv,
    zrecv,
    in_sem,
    blk_sem,
    tab_sem,
    ag_s,
    ag_r,
    far_s,
    far_r,
    seed_s,
    tab_s,
    tab_r,
    sum_s,
    sum_r,
    m_s,
    m_r,
    l_s,
    l_r,
    g_s,
    g_r,
    c_s,
    c_r,
    y_s,
    y_r,
    z_s,
    z_r,
):
    ngx, ngy, nry, nrz, nrc = sizes
    gx, gy, ry, rz, rc = [lax.axis_index(axis) for axis in AXES]
    groups, slots = tiles.shape[0], tiles.shape[1]
    rank, tile = factor.shape
    rows_grp = nry * nrz * nrc
    me = gx * ngy + gy
    far = ngx // 2

    def place(y, z, c):
        return (y * nrz + z) * nrc + c

    mine = place(ry, rz, rc)
    deep = rank // CHUNKS
    half = nrz

    def group_peer(h):
        hx, hy = h // ngy, h % ngy
        flip = (hy - gy) * (hy - gy)
        return (hx, hy, ry + flip - 2 * ry * flip, rz, rc)

    def z_peer(z):
        return (gx, gy, ry, z, rc)

    y_peer = (gx, gy, 1 - ry, rz, rc)
    c_peer = (gx, gy, ry, rz, 1 - rc)

    def z_other(i):
        step = (i // 2 + 1) * (1 - 2 * (i % 2))
        return (rz + step + nrz) % nrz

    def remote(src, dst, send, recv, peer):
        return pltpu.make_async_remote_copy(
            src_ref=src, dst_ref=dst, send_sem=send, recv_sem=recv, device_id=peer, device_id_type=BY_MESH
        )

    def block_copy(h):
        return pltpu.make_async_copy(blocks.at[0, h], tiles.at[h], blk_sem.at[h])

    def loop(start, stop, body):
        def step(i, carry):
            body(i)
            return carry

        lax.fori_loop(start, stop, step, 0)

    cols_copy = pltpu.make_async_copy(cols_in, cols, in_sem.at[0])
    factor_copy = pltpu.make_async_copy(factor_in, factor, in_sem.at[1])
    cols_copy.start()
    factor_copy.start()
    barrier = pltpu.get_barrier_semaphore()

    def greet(peer):
        pl.semaphore_signal(barrier, inc=1, device_id=peer, device_id_type=BY_MESH)

    loop(0, me, lambda h: greet(group_peer(h)))
    loop(me + 1, groups, lambda h: greet(group_peer(h)))
    loop(0, nrz - 1, lambda i: greet(z_peer(z_other(i))))
    greet(y_peer)
    greet(c_peer)
    loop(0, me + 1, lambda h: block_copy(h).start())

    hall[rows_grp] = jnp.zeros((rank, tile), hall.dtype)
    for q in range(ngy):
        hfar[q, rows_grp] = jnp.zeros((rank, tile), hall.dtype)
    for g in range(groups):
        for c in range(CHUNKS):
            recvm[c][g, slots] = jnp.full((deep, tile), -32768, jnp.int32).astype(sendm.dtype)
    for c in range(CHUNKS):
        ownm[c, slots] = jnp.zeros((deep, tile), jnp.float32)
    cols_copy.wait()
    factor_copy.wait()
    hall[mine] = factor[...]
    all_cols = cols[0]
    lane = lax.broadcasted_iota(jnp.int32, (groups, LANES), 1)
    row = lax.broadcasted_iota(jnp.int32, (groups, LANES), 0)
    table = jnp.where(lane >= INV_LANE, slots, rows_grp)
    for s in range(slots):
        column = jnp.broadcast_to(all_cols[:, s : s + 1], (groups, LANES))
        offset = column - row * rows_grp
        live = (offset >= 0) & (offset < rows_grp)
        table = jnp.where(live & (lane == s), offset, table)
        table = jnp.where(live & (lane - INV_LANE == offset), s, table)
    for h in range(groups):
        tab[h] = jnp.broadcast_to(table[h : h + 1], (8, LANES))

    def keep_own(h):
        tabin[h] = tab[h]

    loop(0, me + 1, keep_own)
    row_sums = nt_dot(jnp.ones((8, tile), jnp.bfloat16), factor[...])
    sums[...] = jnp.zeros((8, LANES), jnp.float32)
    sums[:, 0:rank] = jnp.maximum(row_sums, 1e-30)
    to_levels = LEVELS / to_column(sums[0:1, :], rank)

    def mirror_send(h, c):
        return remote(
            sendm.at[h, c], recvm[c].at[me, pl.ds(0, slots)], m_s.at[h, c], m_r.at[me, c], group_peer(h)
        )

    def mirror(h):
        block_copy(h).wait()
        for s in range(slots):
            product = jnp.dot(factor[...], tiles[h, s], preferred_element_type=jnp.float32)
            coded = jnp.round(product * to_levels - OFFSET).astype(jnp.int32).astype(sendm.dtype)
            for c in range(CHUNKS):
                sendm[h, c, s] = coded[c * deep : (c + 1) * deep]

    pl.semaphore_wait(barrier, groups - 1 + nrz - 1 + 2)

    class Gather:
        def __init__(self, held, send, recv, y):
            self.held, self.send, self.recv, self.y = held, send, recv, y
            self.seed = place(y, rz, rc)

        def z_copy(self, z, src):
            p = self.seed
            return remote(src, self.held.at[p], self.send.at[z], self.recv.at[p], z_peer(z))

        def y_copy(self, z, src):
            p = place(self.y, z, rc)
            return remote(src, self.held.at[p], self.send.at[nrz + z], self.recv.at[p], y_peer)

        def c_copy(self, y, z, src):
            p = place(y, z, rc)
            return remote(src, self.held.at[p], self.send.at[(2 + y) * nrz + z], self.recv.at[p], c_peer)

        def arrived(self, p):
            remote(factor, self.held.at[p], self.send.at[0], self.recv.at[p], c_peer).wait_recv()

        def begin(self, src):
            loop(0, nrz - 1, lambda i: self.z_copy(z_other(i), src).start())
            self.y_copy(rz, src).start()
            self.c_copy(self.y, rz, src).start()

        def forward(self, i):
            z = z_other(i)
            p = place(self.y, z, rc)
            self.arrived(p)
            self.y_copy(z, self.held.at[p]).start()
            self.c_copy(self.y, z, self.held.at[p]).start()

        def second(self, i):
            z = (rz + i) % nrz
            p = place(1 - self.y, z, rc)
            self.arrived(p)
            self.c_copy(1 - self.y, z, self.held.at[p]).start()

        def finish(self):
            loop(0, nry * nrz, lambda j: self.arrived(j * nrc + 1 - rc))

        def drain(self):
            loop(0, nrz - 1, lambda i: self.z_copy(z_other(i), factor).wait_send())
            loop(0, nrz, lambda z: self.y_copy(z, factor).wait_send())
            loop(0, nry * nrz, lambda j: self.c_copy(j // nrz, j % nrz, factor).wait_send())

    def flipped(y, q):
        flip = (q - gy) * (q - gy)
        return y + flip - 2 * y * flip

    near_set = Gather(hall, ag_s, ag_r, ry)
    far_sets = [Gather(hfar.at[q], far_s.at[q], far_r.at[q], flipped(ry, q)) for q in range(ngy)]

    def seed_send(q):
        peer = (gx + far, q, flipped(ry, q), rz, rc)
        return remote(factor, hfar.at[gy, mine], seed_s.at[q], far_r.at[gy, mine], peer)

    def when_far(body):
        pl.when(gx >= far)(body)

    near_set.begin(factor)

    @pl.when(gx < far)
    def _():
        for q in range(ngy):
            seed_send(q).start()

    def table_send(h):
        return remote(tab.at[h], tabin.at[me], tab_s.at[h], tab_r.at[me], group_peer(h))

    def sums_send(h):
        return remote(sums, sumsin.at[me], sum_s.at[h], sum_r.at[me], group_peer(h))

    def small_sends(h):
        table_send(h).start()
        sums_send(h).start()

    loop(0, me, small_sends)

    def mirror_late(h):
        mirror(h)
        mirror_send(h, 0).start()

    loop(0, me, mirror_late)
    for chunk in range(1, CHUNKS):
        loop(0, me, lambda h: mirror_send(h, chunk).start())

    block_copy(me).wait()
    for s in range(slots):
        product = jnp.dot(factor[...], tiles[me, s], preferred_element_type=jnp.float32)
        for c in range(CHUNKS):
            ownm[c, s] = product[c * deep : (c + 1) * deep]

    loop(0, nrz - 1, near_set.forward)

    @when_far
    def _():
        for held in far_sets:
            held.arrived(held.seed)
            held.begin(held.held.at[held.seed])

    loop(0, nrz, near_set.second)

    def tables_in(g):
        remote(tab.at[0], tabin.at[g], tab_s.at[0], tab_r.at[g], c_peer).wait_recv()
        remote(sums, sumsin.at[g], sum_s.at[0], sum_r.at[g], c_peer).wait_recv()
        column = to_column(sumsin[g][0:1, :], rank) * (1.0 / LEVELS)
        scale[g] = jnp.broadcast_to(column, (rank, tile))

    loop(me + 1, groups, tables_in)
    to_scalars = pltpu.make_async_copy(tabin, tabs, tab_sem)
    to_scalars.start()
    to_scalars.wait()
    near_set.finish()

    def lower_send(g):
        return remote(sendl.at[g], recvl.at[me], l_s.at[g], l_r.at[me], group_peer(g))

    def serve(g):
        @pl.when(g // ngy != gx + far)
        def _():
            for s in range(slots):
                sendl[g, s] = hall[tabs[g, 0, s]]
            lower_send(g).start()

    loop(me + 1, groups, serve)

    gsend[...] = jnp.zeros((rank, LANES), jnp.float32)

    def gram_part(part_of):
        def step(i, total):
            for p in range(4):
                held = hall[part_of * (rows_grp // 2) + i * 4 + p]
                total += nt_dot(held, held)
            return total

        gsend[:, 0:rank] = lax.fori_loop(0, rows_grp // 8, step, gsend[:, 0:rank])

    def gram_send(h):
        return remote(gsend, grecv.at[me], g_s.at[h], g_r.at[me], group_peer(h))

    def gram_sends():
        grecv[me] = gsend[...]
        loop(0, me, lambda h: gram_send(h).start())
        loop(me + 1, groups, lambda h: gram_send(h).start())

    base[...] = jnp.zeros((rank, tile), jnp.float32)

    def no_scale(g):
        scale[g] = jnp.zeros((rank, tile), jnp.float32)

    loop(0, me + 1, no_scale)
    for g in range(1, groups):
        base[...] += OFFSET * scale[g]
    other, own = (1 - ry) * nrz, ry * nrz

    def core_send(c, y):
        first = pl.ds(y * nrz, half)
        return remote(cbuf.at[c, first], crecv.at[c, first], c_s.at[c, y], c_r.at[c, y], c_peer)

    def row_y_send(c):
        return remote(part.at[c, pl.ds(other, half)], yrecv.at[c], y_s.at[c], y_r.at[c], y_peer)

    def row_z_send(c, z):
        return remote(part.at[c, own + z], zrecv.at[c, rz], z_s.at[c, z], z_r.at[c, rz], z_peer(z))

    def sum_chunk(c):
        rows = slice(c * deep, (c + 1) * deep)

        def mirror_in(g):
            remote(
                sendm.at[0, c], recvm[c].at[g, pl.ds(0, slots)], m_s.at[0, c], m_r.at[g, c], c_peer
            ).wait_recv()

        loop(me + 1, groups, mirror_in)

        def summed(p):
            total = base[rows, :] + ownm[c, tabs[me, 0, INV_LANE + p]]
            for g in range(1, groups):
                slot = jnp.where(g > me, tabs[g, 0, INV_LANE + p], slots)
                total += recvm[c][g, slot].astype(jnp.int32).astype(jnp.float32) * scale[g, rows, :]
            return total

        def for_other_core(j):
            cbuf[c, j] = summed(j * nrc + 1 - rc)

        def for_this_core(j):
            part[c, j] = summed(j * nrc + rc)

        loop(other, other + half, for_other_core)
        core_send(c, 1 - ry).start()
        loop(own, own + half, for_other_core)
        core_send(c, ry).start()
        loop(0, nry * nrz, for_this_core)

    def chunk_to_y(c):
        core_send(c, 1 - ry).wait_recv()

        def add(j):
            part[c, j] += crecv[c, j]

        loop(other, other + half, add)
        row_y_send(c).start()

    def chunk_to_z(c):
        core_send(c, ry).wait_recv()
        row_y_send(c).wait_recv()

        def add(z):
            part[c, own + z] += crecv[c, own + z] + yrecv[c, z]

        def send(i):
            row_z_send(c, z_other(i)).start()

        loop(0, nrz, add)
        loop(0, nrz - 1, send)

    def lower_add(h, tile_of):
        total = lower[...]
        for s in range(slots):
            total += nt_dot(tile_of(s), tiles[h, s])
        lower[...] = total

    for c in range(CHUNKS):
        sum_chunk(c)
        if c == 2:
            lower[...] = jnp.zeros((rank, tile), jnp.float32)
            lower_add(me, lambda s: hall[tabs[me, 0, s]])
        if 1 <= c <= ngy:
            when_far(lambda: loop(0, nrz - 1, far_sets[c - 1].forward))
        if c == 0:
            gram_part(0)
        if c == 1:
            gram_part(1)
            gram_sends()
        if c > 0:
            chunk_to_z(c - 1)
        chunk_to_y(c)
    when_far(lambda: loop(0, nrz, far_sets[0].second))
    chunk_to_z(CHUNKS - 1)
    when_far(lambda: loop(0, nrz, far_sets[1].second))

    @when_far
    def _():
        for held in far_sets:
            held.finish()
        for q in range(ngy):
            h = (gx - far) * ngy + q
            lower_add(h, lambda s: hfar[q, tabs[h, 0, s]])

    def lower_in(h):
        @pl.when(h // ngy != gx - far)
        def _():
            remote(sendl.at[0], recvl.at[h], l_s.at[0], l_r.at[h], c_peer).wait_recv()
            lower_add(h, lambda s: recvl[h, s])

    loop(0, me, lower_in)

    def gram_in(g):
        remote(gsend, grecv.at[g], g_s.at[0], g_r.at[g], c_peer).wait_recv()

    loop(0, me, gram_in)
    loop(me + 1, groups, gram_in)
    total = grecv[0]
    for g in range(1, groups):
        total += grecv[g]
    gram = total[:, 0:rank]

    current = factor[...].astype(jnp.float32)
    fitted = lax.dot_general(
        gram,
        current,
        (((0,), (0,)), ((), ())),
        precision=lax.Precision.HIGHEST,
        preferred_element_type=jnp.float32,
    )
    excess = lower[...] - fitted
    across = lax.broadcasted_iota(jnp.int32, (rank, rank), 1)
    down = lax.broadcasted_iota(jnp.int32, (rank, rank), 0)
    inverse = 1.0 / jnp.sum(jnp.where(across == down, gram, 0.0), axis=1, keepdims=True)
    for chunk in range(CHUNKS):

        def from_z(i):
            z = z_other(i)
            remote(
                part.at[chunk, 0], zrecv.at[chunk, z], z_s.at[chunk, 0], z_r.at[chunk, z], c_peer
            ).wait_recv()
            part[chunk, own + rz] += zrecv[chunk, z]

        loop(0, nrz - 1, from_z)
        begin = chunk * deep % 8
        end = begin + deep
        pieces = [excess[:begin], excess[begin:end] + part[chunk, own + rz], excess[end:]]
        excess = jnp.concatenate([piece for piece in pieces if piece.shape[0]], axis=0)
        for k in range(chunk * deep, (chunk + 1) * deep):
            at = k % 8
            present = current[k : k + 1]
            fresh = jnp.maximum(present + excess[at : at + 1] * inverse[k : k + 1], floor_value)
            out[k : k + 1, :] = fresh
            if k + 1 < rank:
                keep = 8 if at == 7 else 0
                change = fresh - present
                excess = excess[keep:] - gram[k - at + keep :, k : k + 1] * change

    def sent_down(h):
        table_send(h).wait_send()
        sums_send(h).wait_send()
        for c in range(CHUNKS):
            mirror_send(h, c).wait_send()
        gram_send(h).wait_send()

    def sent_up(g):
        gram_send(g).wait_send()

        @pl.when(g // ngy != gx + far)
        def _():
            lower_send(g).wait_send()

    loop(0, me, sent_down)
    loop(me + 1, groups, sent_up)

    def sent_z(i):
        for c in range(CHUNKS):
            row_z_send(c, z_other(i)).wait_send()

    loop(0, nrz - 1, sent_z)
    near_set.drain()

    @pl.when(gx < far)
    def _():
        for q in range(ngy):
            seed_send(q).wait_send()

    @when_far
    def _():
        for held in far_sets:
            held.drain()

    for c in range(CHUNKS):
        row_y_send(c).wait_send()
        for y in range(nry):
            core_send(c, y).wait_send()


def exchange(sizes, blocks, columns, factor):
    _, groups, slots, tile, _ = blocks.shape
    rank = factor.shape[0]
    _, ngy, nry, nrz, nrc = sizes
    rows_grp = nry * nrz * nrc
    pairs = nry * nrz
    f32, bf16, i32, i16 = jnp.float32, jnp.bfloat16, jnp.int32, jnp.int16
    dma = pltpu.SemaphoreType.DMA
    one = (rank, tile)
    deep = (rank // CHUNKS, tile)
    vmem = pl.BlockSpec(memory_space=pltpu.VMEM)
    return pl.pallas_call(
        functools.partial(exchange_kernel, sizes),
        out_shape=jax.ShapeDtypeStruct(one, f32),
        in_specs=[pl.BlockSpec(memory_space=pl.ANY)] * 3,
        out_specs=vmem,
        scratch_shapes=[
            pltpu.VMEM(columns.shape, i32),
            pltpu.VMEM(one, bf16),
            pltpu.VMEM((groups, slots, tile, tile), bf16),
            pltpu.VMEM((rows_grp + 1, *one), bf16),
            pltpu.VMEM((ngy, rows_grp + 1, *one), bf16),
            pltpu.VMEM((groups, 8, LANES), i32),
            pltpu.VMEM((groups, 8, LANES), i32),
            pltpu.SMEM((groups, 8, LANES), i32),
            pltpu.VMEM((8, LANES), f32),
            pltpu.VMEM((groups, 8, LANES), f32),
            pltpu.VMEM((groups, *one), f32),
            pltpu.VMEM(one, f32),
            pltpu.VMEM((groups, CHUNKS, slots, *deep), i16),
            [pltpu.VMEM((groups, slots + 1, *deep), i16)] * CHUNKS,
            pltpu.VMEM((CHUNKS, slots + 1, *deep), f32),
            pltpu.VMEM((groups, slots, *one), bf16),
            pltpu.VMEM((groups, slots, *one), bf16),
            pltpu.VMEM(one, f32),
            pltpu.VMEM((rank, LANES), f32),
            pltpu.VMEM((groups, rank, LANES), f32),
            pltpu.VMEM((CHUNKS, pairs, *deep), f32),
            pltpu.VMEM((CHUNKS, pairs, *deep), f32),
            pltpu.VMEM((CHUNKS, pairs, *deep), f32),
            pltpu.VMEM((CHUNKS, nrz, *deep), f32),
            pltpu.VMEM((CHUNKS, nrz, *deep), f32),
            dma((2,)),
            dma((groups,)),
            dma,
            dma((2 * nrz + pairs,)),
            dma((rows_grp,)),
            dma((ngy, 2 * nrz + pairs)),
            dma((ngy, rows_grp)),
            dma((ngy,)),
            *[dma((groups,))] * 4,
            *[dma((groups, CHUNKS))] * 2,
            *[dma((groups,))] * 4,
            *[dma((CHUNKS, nry))] * 2,
            *[dma((CHUNKS,))] * 2,
            *[dma((CHUNKS, nrz))] * 2,
        ],
        compiler_params=pltpu.CompilerParams(
            collective_id=0, has_side_effects=True, vmem_limit_bytes=48 * 1024 * 1024
        ),
        name="exchange",
    )(blocks, columns, factor)


def solution(mesh):
    groups, rows_grp = mesh.shape["grp"], mesh.shape["row"]
    sizes = (groups // 2, 2, 2, rows_grp // 4, 2)
    split = Mesh(mesh.devices.reshape(sizes), AXES)

    def per_device(blocks, columns, factor):
        return exchange(sizes, blocks, columns, factor)

    placed = (P(AXES, None, None, None, None), P(AXES, None, None), P(None, AXES))
    return jax.shard_map(
        per_device, mesh=split, in_specs=placed, out_specs=P(None, AXES), check_vma=False
    )
```
